32 devices in a mesh: pole: 2 (over x), prow: 8 (over z, y), pcol: 2 (over core).
Axes of the slice: x: 2, y: 2, z: 4, core: 2. Of those that a mesh axis runs over, the one named last changes fastest.
Arguments:
- ancestor_inverse: bfloat16 [8192, 4096], P(('pole', 'prow'), 'pcol'), parts along dimension 0, may hold values from -6 to 6
- l_panel: bfloat16 [8192, 1024], P(('pole', 'prow'), 'pcol'), parts along dimension 0, may hold values from -0.125 to 0.125
- diag_inverse: float32 [2048, 256], P(('pole', 'pcol')), parts along dimension 0, may hold values from -6 to 6
- pattern: int32 [4, 8], replicated, may hold values from 0 to 15, as said below
Outputs:
- column_blocks: float32 [8192, 1024], P(('pole', 'prow'), 'pcol'), parts along dimension 0
- diag_blocks: float32 [2048, 256], P(('pole', 'pcol')), parts along dimension 0
The draws below stay inside these ranges and needn't reach their ends.
There are 2 independent parts, one for each index of `pole`. The reference program is written for one: setup_inputs(seed, part) draws one part's arguments, and reference() takes and returns one part's arrays. A program takes and returns all parts, laid end to end along the dimension named above; an argument that names none is the same for every part. Nothing has to cross between parts.
Inputs may be any that keep to these rules, and one draw needn't show every extreme that they name: `pattern`: each row lists 8 different ancestor supernodes in increasing order, and every row lists ancestor 16 - 1.
All inputs are finite; a program needn't handle non-finite values.
Results may differ from the reference program's by a relative error of at most 0.0003.
Values may be sent and summed in bfloat16 or wider, within the bound.
No kernel may reach another device: no remote copies, remote signals or barrier semaphores. Data moves between devices by JAX's collectives and lax.ppermute only.
A program may use at most 128 MiB of HBM per device.

```python
import jax
import jax.numpy as jnp
import numpy as np
from jax import lax

B = 256
RT = 2
NK = 4
NA = 16
S = 8
N_PCOL = 2


def draw_pattern(key, part):
    scores = jax.random.randint(key, (NK, NA), 0, 2 * NA)
    positions = jnp.arange(NA, dtype=jnp.int32)
    scores = (scores + positions[None, :]) * NA + positions[None, :]
    scores = scores.at[:, NA - 1].set(4 * NA * NA)
    _, chosen = lax.top_k(scores, S)
    return jnp.sort(chosen, axis=1).astype(jnp.int32)


def levels(rng, dims, cuts, least, high):
    level = 1.0
    for axis_at, shards_of in cuts:
        steps = jax.random.uniform(jax.random.fold_in(jax.random.fold_in(rng, 6), axis_at), (shards_of,), jnp.float32, least / len(cuts), high / len(cuts))
        level = level * jnp.repeat(jnp.exp(steps), dims[axis_at] // shards_of).reshape((-1,) + (1,) * (len(dims) - 1 - axis_at))
    return level


def bell_draw(own_key, dims, deviation, reach, cuts=(), kind=jnp.bfloat16):
    result = jax.random.normal(own_key, dims, jnp.float32) * deviation
    if len(cuts) > 0:
        result = levels(own_key, dims, cuts, -0.22, 0.18) * result
    return jnp.clip(result, min=-reach, max=reach).astype(kind)


def setup_inputs(seed: int = 0, part: int = 0) -> dict:
    keys = jax.random.split(jax.random.key(seed), 5)
    own_keys = jax.random.split(jax.random.fold_in(keys[4], part), 5)
    ancestor_inverse = bell_draw(own_keys[0], (NA * B, NA * B), 1.0, 6.0, ((0, 8), (1, 2)))
    l_panel = bell_draw(own_keys[1], (NA * B, NK * B), (S * B) ** -0.5, 0.125, ((0, 8), (1, 2)))
    diag_inverse = bell_draw(own_keys[2], (NK * B, B), 1.0, 6.0, ((0, 2),), jnp.float32)
    pattern = draw_pattern(jax.random.fold_in(keys[4], 71), part)
    return {"ancestor_inverse": ancestor_inverse, "l_panel": l_panel, "diag_inverse": diag_inverse, "pattern": pattern}


def reference(ancestor_inverse, l_panel, diag_inverse, pattern):
    share = RT // N_PCOL
    per_column = NA // N_PCOL
    stored = np.arange(NA)
    column_part = stored // per_column
    remain = stored % per_column
    tile_order = (remain // share) * RT + column_part * share + remain % share
    tile_ids = jnp.arange(NA, dtype=jnp.int32)
    member = jnp.any(pattern[None, :, :] == tile_ids[:, None, None], axis=2).astype(jnp.float32)
    panel_mask = member[:, None, :, None]
    masked = (l_panel.reshape(NA, B, NK, B) * panel_mask.astype(jnp.bfloat16)).reshape(NA * B, NK * B)
    ordered = masked.reshape(NA, B, NK * B)[tile_order].reshape(NA * B, NK * B)
    product_full = -jnp.dot(ancestor_inverse, ordered, preferred_element_type=jnp.float32)
    column_blocks = (product_full.reshape(NA, B, NK, B) * panel_mask).reshape(NA * B, NK * B).astype(jnp.float32)
    diag_terms = jnp.einsum("rkb,rkc->kbc", masked.astype(jnp.float32).reshape(NA * B, NK, B),
                            product_full.reshape(NA * B, NK, B), precision=lax.Precision.HIGHEST)
    diag_blocks = diag_inverse - diag_terms.reshape(NK * B, B)
    return column_blocks, diag_blocks
```

```python
import functools

import jax
import jax.numpy as jnp
from jax import lax
from jax.experimental import pallas as pl
from jax.experimental.pallas import tpu as pltpu
from jax.sharding import PartitionSpec as P

B = 256


def ring_order(mesh):
    n = mesh.shape["prow"]
    natural = list(range(n))
    try:
        at = [tuple(d.coords) for d in mesh.devices[0, :, 0]]
    except AttributeError:
        return natural
    varying = [i for i in range(len(at[0])) if len({c[i] for c in at}) > 1]
    if len(varying) == 2 and n % 2 == 0:
        for axis in varying:
            low = min(c[axis] for c in at)
            if len({c[axis] for c in at}) == 2:
                other = varying[0] if axis == varying[1] else varying[1]
                one = sorted((c[other], i) for i, c in enumerate(at) if c[axis] == low)
                two = sorted((c[other], i) for i, c in enumerate(at) if c[axis] != low)
                return [i for _, i in one] + [i for _, i in reversed(two)]
    return natural


def xor_of(slot, bits):
    total = 0
    for i, bit in enumerate(reversed(bits)):
        if (slot >> i) & 1:
            total ^= bit
    return total


def product_kernel(steps, halves, nodes, tiles, bit_orders, owners, member, row, a_refs, own, got, out, parts, acc, diag):
    acc[...] = jnp.zeros_like(acc)
    share = tiles // halves
    for s in range(steps):
        for i in range(halves):
            owner = owners[i * steps + s]
            for k in range(nodes):
                for j in range(share):
                    t = owner * tiles + i * share + j

                    @pl.when(member[k * (steps * tiles) + t] > 0)
                    def _():
                        if s == 0:
                            block = own[(i * share + j) * B:(i * share + j + 1) * B, k * B:(k + 1) * B]
                        else:
                            block = got[i][k][s - 1][j * B:(j + 1) * B, :]
                        columns = pl.ds(pl.multiple_of((owner * share + j) * B, B), B)
                        acc[:, k * B:(k + 1) * B] += jnp.dot(
                            a_refs[i][:, columns], block, preferred_element_type=jnp.float32
                        )
    me = row[0]
    for k in range(nodes):
        diag[...] = jnp.zeros_like(diag)
        for i in range(tiles):
            rows = slice(i * B, (i + 1) * B)
            cols = slice(k * B, (k + 1) * B)
            inside = member[k * (steps * tiles) + me * tiles + i] > 0

            @pl.when(inside)
            def _():
                value = acc[rows, cols]
                out[rows, cols] = -value
                left = own[rows, cols]
                high = value.astype(jnp.bfloat16)
                rest = value - high.astype(jnp.float32)
                mid = rest.astype(jnp.bfloat16)
                low = (rest - mid.astype(jnp.float32)).astype(jnp.bfloat16)
                total = diag[...]
                for part in (low, mid, high):
                    total += lax.dot_general(
                        left, part, (((0,), (0,)), ((), ())), preferred_element_type=jnp.float32
                    )
                diag[...] = total

            @pl.when(jnp.logical_not(inside))
            def _():
                out[rows, cols] = jnp.zeros((B, B), jnp.float32)

        size = B // steps
        for q in range(steps):
            piece = jnp.bitwise_xor(me, xor_of(q, bit_orders[k % 2]))
            parts[k][q * size:(q + 1) * size, :] = diag[pl.ds(pl.multiple_of(piece * size, size), size), :]


def finish_kernel(steps, nodes, bit_orders, row, base, totals, out):
    size = B // steps
    half = steps // 2
    me = row[0]
    for k in range(nodes):
        for q in range(steps):
            piece = jnp.bitwise_xor(me, xor_of(q, bit_orders[k % 2]))
            at = pl.ds(pl.multiple_of(k * B + piece * size, size), size)
            source = totals[k][q // half]
            out[at, :] = base[at, :] + source[(q % half) * size:(q % half + 1) * size, :]


def per_device(ring, a_own, l_panel, diag_inverse, pattern):
    n = len(ring)
    halves = lax.axis_size("pcol")
    row = lax.axis_index("prow")
    col = lax.axis_index("pcol")
    rows, cols = l_panel.shape
    tiles, nodes = rows // B, cols // B
    h = rows // halves
    at = {r: i for i, r in enumerate(ring)}
    clockwise = [(ring[i], ring[(i + 1) % n]) for i in range(n)]
    counter = [(ring[(i + 1) % n], ring[i]) for i in range(n)]
    swap = [(i, i ^ 1) for i in range(halves)]

    a_other = lax.ppermute(a_own, "pcol", swap)
    got = [[[] for _ in range(nodes)] for _ in range(halves)]
    current = [
        [l_panel[i * h:(i + 1) * h, k * B:(k + 1) * B] for k in range(nodes)] for i in range(halves)
    ]
    for _ in range(n - 1):
        for k in range(nodes):
            for i in range(halves):
                current[i][k] = lax.ppermute(current[i][k], "prow", counter if i % 2 else clockwise)
                got[i][k].append(current[i][k])

    table = jnp.asarray(
        [[ring[(at[r] + (s if i % 2 else -s)) % n] for i in range(halves) for s in range(n)] for r in range(n)],
        jnp.int32,
    )
    owners = lax.dynamic_index_in_dim(table, row, 0, keepdims=False)
    node_rows = lax.dynamic_slice_in_dim(pattern, col * nodes, nodes, 0)
    tile_ids = jnp.arange(n * tiles, dtype=jnp.int32)
    member = jnp.any(node_rows[:, None, :] == tile_ids[None, :, None], axis=2).astype(jnp.int32).reshape(-1)
    row_ref = row.astype(jnp.int32).reshape(1)

    bits = [1 << i for i in range(n.bit_length() - 1)]
    bit_orders = (tuple(bits), tuple([bits[1], bits[0]] + bits[2:]))

    smem = pl.BlockSpec(memory_space=pltpu.SMEM)
    vmem = pl.BlockSpec(memory_space=pltpu.VMEM)
    flat = [g for half in got for node in half for g in node]

    def body(owners, member, row_ref, col_ref, a0, a1, own, *rest):
        blocks, (out, *parts), (acc, diag) = rest[:len(flat)], rest[len(flat):-2], rest[-2:]
        nested = [
            [blocks[(i * nodes + k) * (n - 1):(i * nodes + k + 1) * (n - 1)] for k in range(nodes)]
            for i in range(halves)
        ]
        for c in range(halves):
            @pl.when(col_ref[0] == c)
            def _():
                refs = (a0, a1) if c == 0 else (a1, a0)
                product_kernel(n, halves, nodes, tiles, bit_orders, owners, member, row_ref, refs, own, nested, out, parts, acc, diag)

    column_blocks, *parts = pl.pallas_call(
        body,
        in_specs=[smem] * 4 + [vmem] * (3 + len(flat)),
        out_specs=[vmem] * (1 + nodes),
        out_shape=[jax.ShapeDtypeStruct((rows, cols), jnp.float32)]
        + [jax.ShapeDtypeStruct((B, B), jnp.float32)] * nodes,
        scratch_shapes=[pltpu.VMEM((rows, cols), jnp.float32), pltpu.VMEM((B, B), jnp.float32)],
    )(owners, member, row_ref, col.astype(jnp.int32).reshape(1), a_own, a_other, l_panel, *flat)

    def partner(bit):
        return [(i, i ^ bit) for i in range(n)]

    held = list(parts)
    for step in range(len(bits)):
        size = held[0].shape[0] // 2
        came = [lax.ppermute(held[k][size:], "prow", partner(bit_orders[k % 2][step])) for k in range(nodes)]
        held = [held[k][:size] + came[k] for k in range(nodes)]
    for step in reversed(range(len(bits))):
        came = [lax.ppermute(held[k], "prow", partner(bit_orders[k % 2][step])) for k in range(nodes)]
        if step:
            held = [jnp.concatenate([held[k], came[k]], 0) for k in range(nodes)]
    totals = [(held[k], came[k]) for k in range(nodes)]

    def last(row_ref, base, *rest):
        *pieces, out = rest
        finish_kernel(n, nodes, bit_orders, row_ref, base, [pieces[2 * k:2 * k + 2] for k in range(nodes)], out)

    diag_blocks = pl.pallas_call(
        last,
        in_specs=[smem] + [vmem] * (1 + 2 * nodes),
        out_specs=vmem,
        out_shape=jax.ShapeDtypeStruct(diag_inverse.shape, jnp.float32),
    )(row_ref, diag_inverse, *[piece for pair in totals for piece in pair])
    return column_blocks, diag_blocks


def solution(mesh):
    return jax.shard_map(
        functools.partial(per_device, ring_order(mesh)),
        mesh=mesh,
        in_specs=(
            P(("pole", "prow"), "pcol"),
            P(("pole", "prow"), "pcol"),
            P(("pole", "pcol"), None),
            P(),
        ),
        out_specs=(P(("pole", "prow"), "pcol"), P(("pole", "pcol"), None)),
        check_vma=False,
    )
```
